256 devices in a mesh: tm: 16 (over z, core), space: 16 (over x, y).
Axes of the slice: x: 4, y: 4, z: 8, core: 2. Of those that a mesh axis runs over, the one named last changes fastest.
Arguments:
- initial_state: float32 [128, 128, 128], P('space'), may hold values from -1 to 1
- fine_steps: int32 [16], P('tm'), may hold values from 2 to 8, as said below
- sweep_count: int32 [1], replicated, may hold values from 2 to 4
Outputs:
- end_states: float32 [16, 128, 128, 128], P('tm', 'space')
The draws below stay inside these ranges and needn't reach their ends.
Inputs may be any that keep to these rules, and one draw needn't show every extreme that they name: Slice n takes fine_steps[n] fine steps; some slice takes exactly 8.
All inputs are finite; a program needn't handle non-finite values.
Results may differ from the reference program's by a relative error of at most 0.0001.
Values sent between devices are 32-bit elements; how exact they have to be, the bound alone decides.
A program may use at most 64 MiB of HBM per device.

```python
import jax
import jax.numpy as jnp
from jax import lax

NX = 128
NY = 128
FSTEPS = 8
FMIN = 2
PITERS = 2
SLICES = 16
NZ = 128


def draw_fine_steps(key, part):
    first, second, third = jax.random.split(jax.random.fold_in(key, 11), 3)
    base = jax.random.randint(first, (SLICES,), FMIN, FMIN + 3)
    heavy = jax.random.randint(second, (SLICES,), 0, 8) == 0
    forced = jnp.arange(SLICES) == jax.random.randint(third, (), 0, SLICES)
    return jnp.where(heavy | forced, FSTEPS, base).astype(jnp.int32)


def shard_levels(stream_key, dims, shards, smallest, high):
    factor_of, own = 1.0, jax.random.fold_in(stream_key, 6)
    for axis_at, shards_of in shards:
        draws = jnp.exp(jax.random.uniform(jax.random.fold_in(own, axis_at), (shards_of,), jnp.float32, smallest / len(shards), high / len(shards)))
        factor_of = factor_of * jnp.repeat(draws, dims[axis_at] // shards_of).reshape([-1 if axis == axis_at else 1 for axis in range(len(dims))])
    return factor_of


def setup_inputs(seed: int = 0) -> dict:
    splits = jax.random.split(jax.random.key(seed), 4)
    initial_state = jnp.clip(jax.random.uniform(splits[0], (NZ, NY, NX), jnp.float32, -1.0, 1.0) * shard_levels(splits[0], (NZ, NY, NX), ((0, 16),), -0.4, 0.0), -1.0, 1.0)
    fine_steps = draw_fine_steps(jax.random.fold_in(splits[3], 71), 0)
    sweep_count = jax.random.randint(splits[2], (1,), 2, 5).astype(jnp.int32)
    return {"initial_state": initial_state, "fine_steps": fine_steps, "sweep_count": sweep_count}


SLICE_TIME = 0.6
MOBILITY = 0.5


def planar_sum(field):
    return jnp.roll(field, 1, 1) + jnp.roll(field, -1, 1) + jnp.roll(field, 1, 2) + jnp.roll(field, -1, 2)


def coarse(state, sweeps):
    source = state + SLICE_TIME * (state - state * state * state)
    weight = SLICE_TIME * MOBILITY
    divisor = 1.0 + 4.0 * weight

    def sweep(turn, guess):
        return (source + weight * planar_sum(guess)) / divisor

    return lax.fori_loop(0, sweeps, sweep, source)


def fine_solve(state, step_count):
    step_size = SLICE_TIME / step_count.astype(jnp.float32)

    def single(turn, field):
        neighbours = jnp.roll(field, 1, 0) + jnp.roll(field, -1, 0) + planar_sum(field)
        moved = field + step_size * (MOBILITY * (neighbours - 6.0 * field) + field - field * field * field)
        return jnp.where(turn < step_count, moved, field)

    return lax.fori_loop(0, FSTEPS, single, state)


def reference(initial_state, fine_steps, sweep_count):
    sweeps = sweep_count[0]
    starts = [initial_state]
    for slice_index in range(SLICES - 1):
        starts.append(coarse(starts[slice_index], sweeps))
    finals = starts
    for outer_round in range(PITERS):
        corrections = [fine_solve(starts[slice_index], fine_steps[slice_index]) - coarse(starts[slice_index], sweeps) for slice_index in range(SLICES)]
        updated = [initial_state]
        for slice_index in range(SLICES - 1):
            updated.append(coarse(updated[slice_index], sweeps) + corrections[slice_index])
        finals = [coarse(updated[slice_index], sweeps) + corrections[slice_index] for slice_index in range(SLICES)]
        starts = updated
    return jnp.stack(finals)
```

```python
import functools

import jax
import jax.numpy as jnp
from jax import lax
from jax.experimental import pallas as pl
from jax.experimental.pallas import tpu as pltpu
from jax.sharding import PartitionSpec as P

FSTEPS = 8
SLICE_TIME = 0.6
MOBILITY = 0.5
WEIGHT = SLICE_TIME * MOBILITY
DIVISOR = 1.0 + 4.0 * WEIGHT
LOWEST_SWEEPS = 2
SWEEPS = 4
MESH = pl.DeviceIdType.MESH


def planar_sum(w):
    last = w.shape[0] - 1
    above = jnp.concatenate([w[1:], pltpu.roll(w[:1], 7, 1)], axis=0)
    below = jnp.concatenate([pltpu.roll(w[last:], 1, 1), w[:last]], axis=0)
    lanes = w.shape[2]
    return (above + below) + (pltpu.roll(w, 1, 2) + pltpu.roll(w, lanes - 1, 2))


def kernel(slices, slabs, init_ref, fine_ref, sweep_ref, out_ref,
           field, entry, given, kept, level_coef, sweep_coef,
           halo_send, halo_recv, chain_send, chain_recv):
    pos = lax.axis_index("tm")
    slab = lax.axis_index("space")
    depth = init_ref.shape[0]
    rows = field.shape[2]
    first, last = pos == 0, pos == slices - 1
    up = lax.rem(slab + 1, slabs)
    down = lax.rem(slab + slabs - 1, slabs)

    barrier = pltpu.get_barrier_semaphore()
    after, before = lax.rem(pos + 1, slices), lax.rem(pos + slices - 1, slices)
    for peer in ({"space": up}, {"space": down}, {"tm": after}, {"tm": before}):
        pl.semaphore_signal(barrier, inc=1, device_id=peer, device_id_type=MESH)

    def halo(turn, side, p):
        return pltpu.make_async_remote_copy(
            src_ref=field.at[turn, depth + p],
            dst_ref=field.at[turn, p + side * 2 * depth],
            send_sem=halo_send.at[turn, side, p],
            recv_sem=halo_recv.at[turn, side, p],
            device_id={"space": down if side else up},
            device_id_type=MESH,
        )

    def chain(turn, p):
        return pltpu.make_async_remote_copy(
            src_ref=given.at[turn, p],
            dst_ref=entry.at[p] if turn else field.at[1, depth + p],
            send_sem=chain_send.at[turn, p],
            recv_sem=chain_recv.at[turn, p],
            device_id={"tm": after},
            device_id_type=MESH,
        )

    tile = level_coef.shape[2:]
    count = jnp.full(tile, fine_ref[0], jnp.int32)
    step = SLICE_TIME / count.astype(jnp.float32)
    for level in range(1, FSTEPS + 1):
        h = jnp.where(count >= level, step, 0.0)
        level_coef[level, 0] = 1.0 - 2.0 * h
        level_coef[level, 1] = h
        level_coef[level, 2] = MOBILITY * h
    sweeps = jnp.full(tile, sweep_ref[0], jnp.int32)
    for turn in range(SWEEPS - LOWEST_SWEEPS):
        active = sweeps >= SWEEPS - turn
        sweep_coef[turn, 0] = jnp.where(active, 1.0 / DIVISOR, 1.0)
        sweep_coef[turn, 1] = jnp.where(active, WEIGHT / DIVISOR, 0.0)

    def coarse(v):
        source = v * ((1.0 + SLICE_TIME) - SLICE_TIME * (v * v))
        w = source
        for turn in range(SWEEPS - LOWEST_SWEEPS):
            w = sweep_coef[turn, 0] * source + sweep_coef[turn, 1] * planar_sum(w)
        source = source * (1.0 / DIVISOR)
        for turn in range(LOWEST_SWEEPS):
            w = source + (WEIGHT / DIVISOR) * planar_sum(w)
        return w

    def load(p, carry):
        for j in range(rows):
            field[0, depth + p, j] = init_ref[p, pl.ds(j, 8, stride=rows), :]

        @pl.when(first)
        def _():
            field[1, depth + p] = field[0, depth + p]
            entry[p] = field[0, depth + p]

        return carry

    lax.fori_loop(0, depth, load, 0)

    def start(n, carry):
        def plane(p, carry):
            field[0, depth + 2 * p] = coarse(field[0, depth + 2 * p])
            field[0, depth + 2 * p + 1] = coarse(field[0, depth + 2 * p + 1])
            return carry

        return lax.fori_loop(0, depth // 2, plane, carry)

    lax.fori_loop(0, pos, start, 0)

    pl.semaphore_wait(barrier, 4)

    def greet(i, carry):
        halo(0, 0, depth - 1 - i).start()
        halo(0, 1, i).start()
        return carry

    lax.fori_loop(0, depth, greet, 0)

    def keep(p, carry):
        kept[p] = coarse(field[0, depth + p])
        return carry

    lax.fori_loop(0, depth, keep, 0)

    def fine(turn, level, z):
        past = ((level + 6) // FSTEPS) * (2 - turn + (level + 1) % 2) + turn
        v = field[past, z]
        side = field[past, z - 1] + field[past, z + 1]
        r = planar_sum(v) + side
        field[2 + level % 2, z] = (
            v * (level_coef[level, 0] - level_coef[level, 1] * (v * v)) + level_coef[level, 2] * r
        )

    half = depth // 2

    def diagonal(turn, d, top):
        def both(level, carry):
            fine(turn, level, depth - d + level)
            fine(turn, level, 2 * depth - 1 + d - level)
            return carry

        lax.fori_loop(1, top + 1, both, 0)

    def relay(turn, p, announce):
        @pl.when(pos > 0)
        def _():
            chain(turn, p).wait_recv()

        if turn == 0:
            announce()
            v = field[1, depth + p]
        else:
            v = entry[p]
        g = coarse(v)
        ended = g + (field[2, depth + p] - kept[p])
        if turn == 0:
            kept[p] = g
        given[turn, p] = ended

        @pl.when(pos < slices - 1)
        def _():
            chain(turn, p).start()

        if turn == 1:
            for j in range(rows):
                out_ref[0, p, pl.ds(j, 8, stride=rows), :] = given[1, p, j]

    for turn in range(2):

        def early(i, carry):
            diagonal(turn, i + 2 - half, i + 1)
            return carry

        lax.fori_loop(0, half - 1, early, 0)

        def wait_halo(d):
            halo(turn, 0, depth - d).wait_recv()
            halo(turn, 1, d - 1).wait_recv()

        def growing(d, carry):
            wait_halo(d)
            diagonal(turn, d, d + half - 1)
            return carry

        lax.fori_loop(1, half + 1, growing, 0)

        def late(d, carry):
            wait_halo(d)
            diagonal(turn, d, FSTEPS)
            lower, upper = depth - d, d - 1

            def tell_lower():
                halo(1, 1, lower).start()

                @pl.when(d == half + 1)
                def _():
                    halo(1, 0, lower).start()

            def tell_upper():
                halo(1, 0, upper).start()

                @pl.when(d == half + 1)
                def _():
                    halo(1, 1, upper).start()

            relay(turn, lower, tell_lower)
            relay(turn, upper, tell_upper)
            return carry

        lax.fori_loop(half + 1, depth + 1, late, 0)

        if turn == 0:

            def rest(i, carry):
                halo(1, 0, half - 2 - i).start()
                halo(1, 1, half + 1 + i).start()
                return carry

            lax.fori_loop(0, half - 1, rest, 0)

    def finish(p, carry):
        for turn in range(2):
            for side in range(2):
                halo(turn, side, p).wait_send()

            @pl.when(pos < slices - 1)
            def _():
                chain(turn, p).wait_send()

        return carry

    lax.fori_loop(0, depth, finish, 0)


def local(initial_state, fine_steps, sweep_count):
    slices, slabs = lax.axis_size("tm"), lax.axis_size("space")
    depth, height, width = initial_state.shape
    plane = (height // 8, 8, width)
    return pl.pallas_call(
        functools.partial(kernel, slices, slabs),
        out_shape=jax.ShapeDtypeStruct((1, *initial_state.shape), jnp.float32),
        in_specs=[
            pl.BlockSpec(memory_space=pltpu.VMEM),
            pl.BlockSpec(memory_space=pltpu.SMEM),
            pl.BlockSpec(memory_space=pltpu.SMEM),
        ],
        out_specs=pl.BlockSpec(memory_space=pltpu.VMEM),
        scratch_shapes=[
            pltpu.VMEM((4, 3 * depth, *plane), jnp.float32),
            pltpu.VMEM((depth, *plane), jnp.float32),
            pltpu.VMEM((2, depth, *plane), jnp.float32),
            pltpu.VMEM((depth, *plane), jnp.float32),
            pltpu.VMEM((FSTEPS + 1, 3, *plane[1:]), jnp.float32),
            pltpu.VMEM((SWEEPS - LOWEST_SWEEPS, 2, *plane[1:]), jnp.float32),
            pltpu.SemaphoreType.DMA((2, 2, depth)),
            pltpu.SemaphoreType.DMA((2, 2, depth)),
            pltpu.SemaphoreType.DMA((2, depth)),
            pltpu.SemaphoreType.DMA((2, depth)),
        ],
        compiler_params=pltpu.CompilerParams(
            collective_id=0, has_side_effects=True, vmem_limit_bytes=48 * 1024 * 1024
        ),
    )(initial_state, fine_steps, sweep_count)


def solution(mesh):
    placed = (P("space", None, None), P("tm"), P())
    return jax.shard_map(
        local, mesh=mesh, in_specs=placed, out_specs=P("tm", "space", None, None), check_vma=False
    )
```

```python
import functools

import jax
import jax.numpy as jnp
from jax import lax
from jax.experimental import pallas as pl
from jax.experimental.pallas import tpu as pltpu
from jax.sharding import PartitionSpec as P

FSTEPS = 8
SLICE_TIME = 0.6
MOBILITY = 0.5
WEIGHT = SLICE_TIME * MOBILITY
DIVISOR = 1.0 + 4.0 * WEIGHT
LOWEST_SWEEPS = 2
SWEEPS = 4
MESH = pl.DeviceIdType.MESH


def planar_sum(w):
    lanes = w[0].shape[1]
    above = w[1:] + [pltpu.roll(w[0], 7, 0)]
    below = [pltpu.roll(w[-1], 1, 0)] + w[:-1]
    return [
        (pltpu.roll(w[j], 1, 1) + pltpu.roll(w[j], lanes - 1, 1)) + (above[j] + below[j])
        for j in range(len(w))
    ]


def kernel(slices, slabs, init_ref, fine_ref, sweep_ref, out_ref,
           field, state, solved, kept, final, level_coef, sweep_coef,
           halo_send, halo_recv, chain_send, chain_recv, pair_send, pair_recv):
    pos = lax.axis_index("tm")
    slab = lax.axis_index("space")
    chip, core = pos // 2, pos % 2
    chips = slices // 2
    depth = init_ref.shape[0]
    half = depth // 2
    rows = field.shape[2]

    barrier = pltpu.get_barrier_semaphore()
    peers = (
        {"space": (slab + 1) % slabs},
        {"space": (slab + slabs - 1) % slabs},
        {"tm": pos + 1 - 2 * core},
        {"tm": (pos + 2) % slices},
        {"tm": (pos + slices - 2) % slices},
    )
    for peer in peers:
        pl.semaphore_signal(barrier, inc=1, device_id=peer, device_id_type=MESH)

    def mine(i):
        return half - 1 - i + core * (1 + 2 * i)

    def theirs(i):
        return half + i - core * (1 + 2 * i)

    def halo(turn, side, p):
        return pltpu.make_async_remote_copy(
            src_ref=field.at[turn, depth + p],
            dst_ref=field.at[turn, p + side * (2 * depth)],
            send_sem=halo_send.at[turn, side, p],
            recv_sem=halo_recv.at[turn, side, p],
            device_id={"space": (slab + 1 + side * (slabs - 2)) % slabs},
            device_id_type=MESH,
        )

    def chain(turn, i):
        return pltpu.make_async_remote_copy(
            src_ref=state.at[1 + turn, 2, i],
            dst_ref=state.at[1 + turn, 0, i],
            send_sem=chain_send.at[turn, i],
            recv_sem=chain_recv.at[turn, i],
            device_id={"tm": (pos + 2) % slices},
            device_id_type=MESH,
        )

    def pair(kind, src, dst, i):
        return pltpu.make_async_remote_copy(
            src_ref=src,
            dst_ref=dst,
            send_sem=pair_send.at[kind, i],
            recv_sem=pair_recv.at[kind, i],
            device_id={"tm": pos + 1 - 2 * core},
            device_id_type=MESH,
        )

    def share(turn, i):
        return pair(turn, state.at[turn, 1 - core, i], field.at[turn, depth + mine(i)], i)

    def share_solved(turn, i):
        return pair(2 + turn, field.at[2, depth + theirs(i)], solved.at[turn, core, i], i)

    def share_final(i):
        return pair(4, state.at[2, 2 - core, i], final.at[i], i)

    tile = level_coef.shape[2:]
    count = jnp.full(tile, fine_ref[0], jnp.int32)
    step = SLICE_TIME / count.astype(jnp.float32)
    for level in range(1, FSTEPS + 1):
        h = jnp.where(count >= level, step, 0.0)
        level_coef[level, 0] = 1.0 - 2.0 * h
        level_coef[level, 1] = h
        level_coef[level, 2] = MOBILITY * h
    sweeps = jnp.full(tile, sweep_ref[0], jnp.int32)
    for power in range(SWEEPS + 1):
        factor = (WEIGHT / DIVISOR) ** power
        inner = jnp.where(sweeps > power, factor / DIVISOR, 0.0)
        sweep_coef[power] = jnp.where(sweeps == power, factor, inner)

    def get(ref, *at):
        return [ref[(*at, j)] for j in range(rows)]

    def put(ref, values, *at):
        for j in range(rows):
            ref[(*at, j)] = values[j]

    def coarse(v):
        power = [x * ((1.0 + SLICE_TIME) - SLICE_TIME * (x * x)) for x in v]
        total = [sweep_coef[0] * x for x in power]
        for turn in range(SWEEPS):
            power = planar_sum(power)
            total = [t + sweep_coef[turn + 1] * x for t, x in zip(total, power)]
        return total

    def load(i, carry):
        for j in range(rows):
            state[0, 0, i, j] = init_ref[mine(i), pl.ds(j, 8, stride=rows), :]

        @pl.when(chip == 0)
        def _():
            state[1, 0, i] = state[0, 0, i]
            state[2, 0, i] = state[0, 0, i]

        return carry

    lax.fori_loop(0, half, load, 0)

    def start(n, carry):
        def plane(i, carry):
            put(state, coarse(get(state, 0, 0, i)), 0, 0, i)
            return carry

        return lax.fori_loop(0, half, plane, carry)

    lax.fori_loop(0, 2 * chip, start, 0)
    pl.semaphore_wait(barrier, len(peers))

    def deal(t, carry):
        i = half - 1 - t
        g = coarse(get(state, 0, 0, i))
        put(state, g, 0, 1, i)
        share(0, i).start()
        put(kept, g, 0, i)
        put(field, get(state, 0, core, i), 0, depth + mine(i))
        halo(0, 1 - core, mine(i)).start()
        return carry

    lax.fori_loop(0, half, deal, 0)

    def greet(t, carry):
        i = half - 1 - t
        share(0, i).wait_recv()
        halo(0, core, theirs(i)).start()
        return carry

    lax.fori_loop(0, half, greet, 0)

    def rest(turn):
        def body(i, carry):
            halo(turn, 0, half - 1 - i).start()
            halo(turn, 1, half + i).start()
            return carry

        lax.fori_loop(0, half, body, 0)

    rest(0)

    def keep(i, carry):
        put(kept, coarse(get(state, 0, 1, i)), 1, i)
        return carry

    lax.fori_loop(0, half, keep, 0)

    def fine(turn, level, z):
        past = ((level + 6) // FSTEPS) * (2 - turn + (level + 1) % 2) + turn
        v = get(field, past, z)
        r = planar_sum(v)
        a, h, b = level_coef[level, 0], level_coef[level, 1], level_coef[level, 2]
        for j in range(rows):
            around = r[j] + (field[past, z - 1, j] + field[past, z + 1, j])
            field[2 + level % 2, z, j] = v[j] * (a - h * (v[j] * v[j])) + b * around

    def diagonal(turn, d, top):
        def both(level, carry):
            fine(turn, level, depth - d + level)
            fine(turn, level, 2 * depth - 1 + d - level)
            return carry

        lax.fori_loop(1, top + 1, both, 0)

    def wait_halo(turn, d):
        halo(turn, 0, depth - d).wait_recv()
        halo(turn, 1, d - 1).wait_recv()

    def finish(turn, i):
        wait_halo(turn, half + 1 + i)
        diagonal(turn, half + 1 + i, FSTEPS)
        share_solved(turn, i).start()
        put(solved, get(field, 2, depth + mine(i)), turn, core, i)

    def relay(turn, i):
        @pl.when(chip > 0)
        def _():
            chain(turn, i).wait_recv()

        g = coarse(get(state, 1 + turn, 0, i))
        share_solved(turn, i).wait_recv()
        for j in range(rows):
            state[1 + turn, 1, i, j] = g[j] + (solved[turn, 0, i, j] - kept[0, i, j])
        if turn == 0:
            put(kept, g, 0, i)
            share(1, i).start()
        g = coarse(get(state, 1 + turn, 1, i))
        for j in range(rows):
            state[1 + turn, 2, i, j] = g[j] + (solved[turn, 1, i, j] - kept[1, i, j])

        @pl.when(chip < chips - 1)
        def _():
            chain(turn, i).start()

        if turn == 0:
            put(kept, g, 1, i)
            put(field, get(state, 1, core, i), 1, depth + mine(i))
            halo(1, 1 - core, mine(i)).start()
        else:
            share_final(i).start()
            for j in range(rows):
                out_ref[0, mine(i), pl.ds(j, 8, stride=rows), :] = state[2, 1 + core, i, j]

    def tell(i):
        share(1, i).wait_recv()
        halo(1, core, theirs(i)).start()

    for turn in range(2):

        def early(i, carry):
            diagonal(turn, i + 2 - half, i + 1)
            return carry

        lax.fori_loop(0, half - 1, early, 0)

        def growing(d, carry):
            wait_halo(turn, d)
            diagonal(turn, d, d + half - 1)
            return carry

        lax.fori_loop(1, half + 1, growing, 0)
        finish(turn, 0)

        def late(i, carry):
            finish(turn, i)
            relay(turn, i - 1)
            if turn == 0:

                @pl.when(i > 1)
                def _():
                    tell(i - 2)

            return carry

        lax.fori_loop(1, half, late, 0)
        if turn == 0:
            tell(half - 2)
        relay(turn, half - 1)
        if turn == 0:
            tell(half - 1)
            rest(1)

            def sent(i, carry):
                share_solved(0, i).wait_send()
                return carry

            lax.fori_loop(0, half, sent, 0)

    def gather(i, carry):
        share_final(i).wait_recv()
        for j in range(rows):
            out_ref[0, theirs(i), pl.ds(j, 8, stride=rows), :] = final[i, j]
        return carry

    lax.fori_loop(0, half, gather, 0)

    def drain(i, carry):
        for turn in range(2):
            for side in range(2):
                halo(turn, side, i).wait_send()
                halo(turn, side, half + i).wait_send()

            @pl.when(chip < chips - 1)
            def _():
                chain(turn, i).wait_send()

            share(turn, i).wait_send()
        share_solved(1, i).wait_send()
        share_final(i).wait_send()
        return carry

    lax.fori_loop(0, half, drain, 0)


def local(initial_state, fine_steps, sweep_count):
    slices, slabs = lax.axis_size("tm"), lax.axis_size("space")
    depth, height, width = initial_state.shape
    plane = (height // 8, 8, width)
    half = depth // 2
    return pl.pallas_call(
        functools.partial(kernel, slices, slabs),
        out_shape=jax.ShapeDtypeStruct((1, *initial_state.shape), jnp.float32),
        in_specs=[
            pl.BlockSpec(memory_space=pltpu.VMEM),
            pl.BlockSpec(memory_space=pltpu.SMEM),
            pl.BlockSpec(memory_space=pltpu.SMEM),
        ],
        out_specs=pl.BlockSpec(memory_space=pltpu.VMEM),
        scratch_shapes=[
            pltpu.VMEM((4, 3 * depth, *plane), jnp.float32),
            pltpu.VMEM((3, 3, half, *plane), jnp.float32),
            pltpu.VMEM((2, 2, half, *plane), jnp.float32),
            pltpu.VMEM((2, half, *plane), jnp.float32),
            pltpu.VMEM((half, *plane), jnp.float32),
            pltpu.VMEM((FSTEPS + 1, 3, *plane[1:]), jnp.float32),
            pltpu.VMEM((SWEEPS + 1, *plane[1:]), jnp.float32),
            pltpu.SemaphoreType.DMA((2, 2, depth)),
            pltpu.SemaphoreType.DMA((2, 2, depth)),
            pltpu.SemaphoreType.DMA((2, half)),
            pltpu.SemaphoreType.DMA((2, half)),
            pltpu.SemaphoreType.DMA((5, half)),
            pltpu.SemaphoreType.DMA((5, half)),
        ],
        compiler_params=pltpu.CompilerParams(
            collective_id=0, has_side_effects=True, vmem_limit_bytes=48 * 1024 * 1024
        ),
    )(initial_state, fine_steps, sweep_count)


def solution(mesh):
    placed = (P("space", None, None), P("tm"), P())
    return jax.shard_map(
        local, mesh=mesh, in_specs=placed, out_specs=P("tm", "space", None, None), check_vma=False
    )
```

```python
import functools

import jax
import jax.numpy as jnp
from jax import lax
from jax.experimental import pallas as pl
from jax.experimental.pallas import tpu as pltpu
from jax.sharding import PartitionSpec as P

FSTEPS = 8
SLICE_TIME = 0.6
MOBILITY = 0.5
WEIGHT = SLICE_TIME * MOBILITY
DIVISOR = 1.0 + 4.0 * WEIGHT
LOWEST_SWEEPS = 2
SWEEPS = 4
MESH = pl.DeviceIdType.MESH


def planar_sum(w):
    lanes = w[0].shape[1]
    above = w[1:] + [pltpu.roll(w[0], 7, 0)]
    below = [pltpu.roll(w[-1], 1, 0)] + w[:-1]
    return [
        (pltpu.roll(w[j], 1, 1) + pltpu.roll(w[j], lanes - 1, 1)) + (above[j] + below[j])
        for j in range(len(w))
    ]


def kernel(slices, slabs, init_ref, fine_ref, sweep_ref, out_ref,
           field, state, solved, kept, final, level_coef, sweep_coef,
           halo_send, halo_recv, chain_send, chain_recv, pair_send, pair_recv):
    pos = lax.axis_index("tm")
    slab = lax.axis_index("space")
    chip, core = pos // 2, pos % 2
    chips = slices // 2
    depth = init_ref.shape[0]
    half = depth // 2
    rows = field.shape[2]

    barrier = pltpu.get_barrier_semaphore()
    peers = (
        {"space": (slab + 1) % slabs},
        {"space": (slab + slabs - 1) % slabs},
        {"tm": pos + 1 - 2 * core},
        {"tm": (pos + 2) % slices},
        {"tm": (pos + slices - 2) % slices},
    )
    for peer in peers:
        pl.semaphore_signal(barrier, inc=1, device_id=peer, device_id_type=MESH)

    def mine(i):
        return half - 1 - i + core * (1 + 2 * i)

    def theirs(i):
        return half + i - core * (1 + 2 * i)

    def halo(turn, side, p):
        return pltpu.make_async_remote_copy(
            src_ref=field.at[turn, depth + p],
            dst_ref=field.at[turn, p + side * (2 * depth)],
            send_sem=halo_send.at[turn, side, p],
            recv_sem=halo_recv.at[turn, side, p],
            device_id={"space": (slab + 1 + side * (slabs - 2)) % slabs},
            device_id_type=MESH,
        )

    def chain(turn, i):
        return pltpu.make_async_remote_copy(
            src_ref=state.at[1 + turn, 2, i],
            dst_ref=state.at[1 + turn, 0, i],
            send_sem=chain_send.at[turn, i],
            recv_sem=chain_recv.at[turn, i],
            device_id={"tm": (pos + 2) % slices},
            device_id_type=MESH,
        )

    def pair(kind, src, dst, i):
        return pltpu.make_async_remote_copy(
            src_ref=src,
            dst_ref=dst,
            send_sem=pair_send.at[kind, i],
            recv_sem=pair_recv.at[kind, i],
            device_id={"tm": pos + 1 - 2 * core},
            device_id_type=MESH,
        )

    def share(turn, i):
        return pair(turn, state.at[turn, 1 - core, i], field.at[turn, depth + mine(i)], i)

    def share_solved(turn, i):
        return pair(2 + turn, field.at[2, depth + theirs(i)], solved.at[turn, core, i], i)

    def share_final(i):
        return pair(4, state.at[2, 2 - core, i], final.at[i], i)

    tile = level_coef.shape[2:]
    count = jnp.full(tile, fine_ref[0], jnp.int32)
    step = SLICE_TIME / count.astype(jnp.float32)
    for level in range(1, FSTEPS + 1):
        h = jnp.where(count >= level, step, 0.0)
        level_coef[level, 0] = 1.0 - 2.0 * h
        level_coef[level, 1] = h
        level_coef[level, 2] = MOBILITY * h
    sweeps = jnp.full(tile, sweep_ref[0], jnp.int32)
    for power in range(SWEEPS + 1):
        factor = (WEIGHT / DIVISOR) ** power
        inner = jnp.where(sweeps > power, factor / DIVISOR, 0.0)
        sweep_coef[power] = jnp.where(sweeps == power, factor, inner)

    def get(ref, *at):
        return [ref[(*at, j)] for j in range(rows)]

    def put(ref, values, *at):
        for j in range(rows):
            ref[(*at, j)] = values[j]

    def coarse(v):
        power = [x * ((1.0 + SLICE_TIME) - SLICE_TIME * (x * x)) for x in v]
        total = [sweep_coef[0] * x for x in power]
        for turn in range(SWEEPS):
            power = planar_sum(power)
            total = [t + sweep_coef[turn + 1] * x for t, x in zip(total, power)]
        return total

    def load(i, carry):
        for j in range(rows):
            state[0, 0, i, j] = init_ref[mine(i), pl.ds(j, 8, stride=rows), :]

        @pl.when(chip == 0)
        def _():
            state[1, 0, i] = state[0, 0, i]
            state[2, 0, i] = state[0, 0, i]

        return carry

    lax.fori_loop(0, half, load, 0)

    def start(n, carry):
        def plane(i, carry):
            put(state, coarse(get(state, 0, 0, i)), 0, 0, i)
            return carry

        return lax.fori_loop(0, half, plane, carry)

    lax.fori_loop(0, 2 * chip, start, 0)
    pl.semaphore_wait(barrier, len(peers))

    def deal(t, carry):
        i = half - 1 - t
        g = coarse(get(state, 0, 0, i))
        put(state, g, 0, 1, i)
        share(0, i).start()
        put(kept, g, 0, i)
        put(field, get(state, 0, core, i), 0, depth + mine(i))
        halo(0, 1 - core, mine(i)).start()
        return carry

    lax.fori_loop(0, half, deal, 0)

    def greet(t, carry):
        i = half - 1 - t
        share(0, i).wait_recv()
        halo(0, core, theirs(i)).start()
        return carry

    lax.fori_loop(0, half, greet, 0)

    def rest(turn):
        def body(i, carry):
            halo(turn, 0, half - 1 - i).start()
            halo(turn, 1, half + i).start()
            return carry

        lax.fori_loop(0, half, body, 0)

    rest(0)

    def keep(i, carry):
        put(kept, coarse(get(state, 0, 1, i)), 1, i)
        return carry

    lax.fori_loop(0, half, keep, 0)

    def fine(turn, level, z):
        past = ((level + 6) // FSTEPS) * (2 - turn + (level + 1) % 2) + turn
        v = get(field, past, z)
        r = planar_sum(v)
        a, h, b = level_coef[level, 0], level_coef[level, 1], level_coef[level, 2]
        r = [x + (y + z) for x, y, z in zip(r, get(field, past, z - 1), get(field, past, z + 1))]
        return [x * (a - h * (x * x)) + b * y for x, y in zip(v, r)]

    def diagonal(turn, d, top):
        def both(level, carry):
            low, high = depth - d + level, 2 * depth - 1 + d - level
            below, above = fine(turn, level, low), fine(turn, level, high)
            put(field, below, 2 + level % 2, low)
            put(field, above, 2 + level % 2, high)
            return carry

        lax.fori_loop(1, top + 1, both, 0)

    def wait_halo(turn, d):
        halo(turn, 0, depth - d).wait_recv()
        halo(turn, 1, d - 1).wait_recv()

    def finish(turn, i):
        wait_halo(turn, half + 1 + i)
        diagonal(turn, half + 1 + i, FSTEPS)
        share_solved(turn, i).start()
        put(solved, get(field, 2, depth + mine(i)), turn, core, i)

    def relay(turn, i):
        @pl.when(chip > 0)
        def _():
            chain(turn, i).wait_recv()

        g = coarse(get(state, 1 + turn, 0, i))
        share_solved(turn, i).wait_recv()
        jump = zip(g, get(solved, turn, 0, i), get(kept, 0, i))
        put(state, [x + (y - z) for x, y, z in jump], 1 + turn, 1, i)
        if turn == 0:
            put(kept, g, 0, i)
            share(1, i).start()
        g = coarse(get(state, 1 + turn, 1, i))
        jump = zip(g, get(solved, turn, 1, i), get(kept, 1, i))
        put(state, [x + (y - z) for x, y, z in jump], 1 + turn, 2, i)

        @pl.when(chip < chips - 1)
        def _():
            chain(turn, i).start()

        if turn == 0:
            put(kept, g, 1, i)
            put(field, get(state, 1, core, i), 1, depth + mine(i))
            halo(1, 1 - core, mine(i)).start()
        else:
            share_final(i).start()
            for j in range(rows):
                out_ref[0, mine(i), pl.ds(j, 8, stride=rows), :] = state[2, 1 + core, i, j]

    def tell(i):
        share(1, i).wait_recv()
        halo(1, core, theirs(i)).start()

    for turn in range(2):

        def early(i, carry):
            diagonal(turn, i + 2 - half, i + 1)
            return carry

        lax.fori_loop(0, half - 1, early, 0)

        def growing(d, carry):
            wait_halo(turn, d)
            diagonal(turn, d, d + half - 1)
            return carry

        lax.fori_loop(1, half + 1, growing, 0)
        finish(turn, 0)

        def late(i, carry):
            finish(turn, i)
            relay(turn, i - 1)
            if turn == 0:

                @pl.when(i > 1)
                def _():
                    tell(i - 2)

            return carry

        lax.fori_loop(1, half, late, 0)
        if turn == 0:
            tell(half - 2)
        relay(turn, half - 1)
        if turn == 0:
            tell(half - 1)
            rest(1)

            def sent(i, carry):
                share_solved(0, i).wait_send()
                return carry

            lax.fori_loop(0, half, sent, 0)

    def gather(i, carry):
        share_final(i).wait_recv()
        for j in range(rows):
            out_ref[0, theirs(i), pl.ds(j, 8, stride=rows), :] = final[i, j]
        return carry

    lax.fori_loop(0, half, gather, 0)

    def drain(i, carry):
        for turn in range(2):
            for side in range(2):
                halo(turn, side, i).wait_send()
                halo(turn, side, half + i).wait_send()

            @pl.when(chip < chips - 1)
            def _():
                chain(turn, i).wait_send()

            share(turn, i).wait_send()
        share_solved(1, i).wait_send()
        share_final(i).wait_send()
        return carry

    lax.fori_loop(0, half, drain, 0)


def local(initial_state, fine_steps, sweep_count):
    slices, slabs = lax.axis_size("tm"), lax.axis_size("space")
    depth, height, width = initial_state.shape
    plane = (height // 8, 8, width)
    half = depth // 2
    return pl.pallas_call(
        functools.partial(kernel, slices, slabs),
        out_shape=jax.ShapeDtypeStruct((1, *initial_state.shape), jnp.float32),
        in_specs=[
            pl.BlockSpec(memory_space=pltpu.VMEM),
            pl.BlockSpec(memory_space=pltpu.SMEM),
            pl.BlockSpec(memory_space=pltpu.SMEM),
        ],
        out_specs=pl.BlockSpec(memory_space=pltpu.VMEM),
        scratch_shapes=[
            pltpu.VMEM((4, 3 * depth, *plane), jnp.float32),
            pltpu.VMEM((3, 3, half, *plane), jnp.float32),
            pltpu.VMEM((2, 2, half, *plane), jnp.float32),
            pltpu.VMEM((2, half, *plane), jnp.float32),
            pltpu.VMEM((half, *plane), jnp.float32),
            pltpu.VMEM((FSTEPS + 1, 3, *plane[1:]), jnp.float32),
            pltpu.VMEM((SWEEPS + 1, *plane[1:]), jnp.float32),
            pltpu.SemaphoreType.DMA((2, 2, depth)),
            pltpu.SemaphoreType.DMA((2, 2, depth)),
            pltpu.SemaphoreType.DMA((2, half)),
            pltpu.SemaphoreType.DMA((2, half)),
            pltpu.SemaphoreType.DMA((5, half)),
            pltpu.SemaphoreType.DMA((5, half)),
        ],
        compiler_params=pltpu.CompilerParams(
            collective_id=0, has_side_effects=True, vmem_limit_bytes=48 * 1024 * 1024
        ),
    )(initial_state, fine_steps, sweep_count)


def solution(mesh):
    placed = (P("space", None, None), P("tm"), P())
    return jax.shard_map(
        local, mesh=mesh, in_specs=placed, out_specs=P("tm", "space", None, None), check_vma=False
    )
```

```python
import functools

import jax
import jax.numpy as jnp
from jax import lax
from jax.experimental import pallas as pl
from jax.experimental.pallas import tpu as pltpu
from jax.sharding import PartitionSpec as P

FSTEPS = 8
SLICE_TIME = 0.6
MOBILITY = 0.5
WEIGHT = SLICE_TIME * MOBILITY
DIVISOR = 1.0 + 4.0 * WEIGHT
LOWEST_SWEEPS = 2
SWEEPS = 4
MESH = pl.DeviceIdType.MESH


def planar_sum(w):
    last, lanes = w.shape[0] - 1, w.shape[2]
    above = jnp.concatenate([w[1:], pltpu.roll(w[:1], 7, 1)], axis=0)
    below = jnp.concatenate([pltpu.roll(w[last:], 1, 1), w[:last]], axis=0)
    return (above + below) + (pltpu.roll(w, 1, 2) + pltpu.roll(w, lanes - 1, 2))


def kernel(slices, slabs, init_ref, fine_ref, sweep_ref, out_ref,
           fetched, level0, odd, even, intake_planes, state, solved, kept, final, level_coef, sweep_coef, fetch_sem,
           halo_send, halo_recv, chain_send, chain_recv, pair_send, pair_recv,
           side_send, side_recv):
    pos = lax.axis_index("tm")
    slab = lax.axis_index("space")
    chip, core = pos // 2, pos % 2
    chips = slices // 2
    depth = init_ref.shape[0]
    half = depth // 2
    rows = even.shape[1]
    other = pos + 1 - 2 * core

    barrier = pltpu.get_barrier_semaphore()
    above, below = (slab + 1) % slabs, (slab + slabs - 1) % slabs
    peers = (
        {"space": above},
        {"space": below},
        {"space": above, "tm": other},
        {"space": below, "tm": other},
        {"tm": other},
        {"tm": (pos + 2) % slices},
        {"tm": (pos + slices - 2) % slices},
    )
    for peer in peers:
        pl.semaphore_signal(barrier, inc=1, device_id=peer, device_id_type=MESH)

    fetch = pltpu.make_async_copy(init_ref.at[pl.ds(half * core, half)], fetched, fetch_sem)
    fetch.start()

    def mine(i):
        return half - 1 - i + core * (1 + 2 * i)

    def theirs(i):
        return half + i - core * (1 + 2 * i)

    def halo(turn, side, piece, i):
        p = mine(i)
        if turn == 0:
            target, core_there = intake_planes.at[depth - 1 - p + side * (2 * p + 1 - depth), 0], side
        else:
            target, core_there = level0.at[1, p + side * (2 * depth)], piece
        return pltpu.make_async_remote_copy(
            src_ref=state.at[turn, piece, i],
            dst_ref=target,
            send_sem=halo_send.at[turn, side, piece, i],
            recv_sem=halo_recv.at[turn, side, p],
            device_id={
                "space": (slab + 1 + side * (slabs - 2)) % slabs,
                "tm": 2 * chip + core_there,
            },
            device_id_type=MESH,
        )

    def wait_side(turn, side, p):
        pltpu.make_async_remote_copy(
            src_ref=state.at[turn, core, 0],
            dst_ref=state.at[turn, core, 0],
            send_sem=halo_send.at[turn, side, 0, 0],
            recv_sem=halo_recv.at[turn, side, p],
            device_id={"space": (slab + 1 + side * (slabs - 2)) % slabs},
            device_id_type=MESH,
        ).wait_recv()

    def share_side(d):
        return pltpu.make_async_remote_copy(
            src_ref=intake_planes.at[d - 1, 1 - core],
            dst_ref=level0.at[0, depth - d + core * (depth + 2 * d - 1)],
            send_sem=side_send.at[d - 1],
            recv_sem=side_recv.at[d - 1],
            device_id={"tm": other},
            device_id_type=MESH,
        )

    def chain(turn, i):
        return pltpu.make_async_remote_copy(
            src_ref=state.at[1 + turn, 2, i],
            dst_ref=state.at[1 + turn, 0, i],
            send_sem=chain_send.at[turn, i],
            recv_sem=chain_recv.at[turn, i],
            device_id={"tm": (pos + 2) % slices},
            device_id_type=MESH,
        )

    def pair(kind, src, dst, i):
        return pltpu.make_async_remote_copy(
            src_ref=src,
            dst_ref=dst,
            send_sem=pair_send.at[kind, i],
            recv_sem=pair_recv.at[kind, i],
            device_id={"tm": other},
            device_id_type=MESH,
        )

    def share(turn, i):
        return pair(turn, state.at[turn, 1 - core, i], level0.at[turn, depth + mine(i)], i)

    def share_solved(turn, i):
        return pair(2 + turn, even.at[depth + theirs(i)], solved.at[turn, core, i], i)

    def share_final(i):
        return pair(4, state.at[2, 2 - core, i], final.at[i], i)

    tile = level_coef.shape[2:]
    count = jnp.full(tile, fine_ref[0], jnp.int32)
    step = SLICE_TIME / count.astype(jnp.float32)
    for level in range(1, FSTEPS + 1):
        h = jnp.where(count >= level, step, 0.0)
        level_coef[level, 0] = 1.0 - 2.0 * h
        level_coef[level, 1] = h
        level_coef[level, 2] = MOBILITY * h
    sweeps = jnp.full(tile, sweep_ref[0], jnp.int32)
    for power in range(SWEEPS + 1):
        factor = (WEIGHT / DIVISOR) ** power
        inner = jnp.where(sweeps > power, factor / DIVISOR, 0.0)
        sweep_coef[power] = jnp.where(sweeps == power, factor, inner)

    def coarse(v):
        power = v * ((1.0 + SLICE_TIME) - SLICE_TIME * (v * v))
        total = sweep_coef[0] * power
        for turn in range(SWEEPS):
            power = planar_sum(power)
            total = total + sweep_coef[turn + 1] * power
        return total

    def load(i, carry):
        for j in range(rows):
            state[0, 0, i, j] = fetched[mine(i) - half * core, pl.ds(j, 8, stride=rows), :]

        @pl.when(chip == 0)
        def _():
            state[1, 0, i] = state[0, 0, i]
            state[2, 0, i] = state[0, 0, i]

        return carry

    fetch.wait()
    lax.fori_loop(0, half, load, 0)

    def start(n, carry):
        def plane(i, carry):
            state[0, 0, i] = coarse(state[0, 0, i])
            return carry

        return lax.fori_loop(0, half, plane, carry)

    lax.fori_loop(0, 2 * chip, start, 0)
    def deal(i, carry):
        g = coarse(state[0, 0, i])
        state[0, 1, i] = g
        kept[0, i] = g
        level0[0, depth + mine(i)] = state[0, core, i]
        kept[1, i] = coarse(g)
        return carry

    lax.fori_loop(0, half, deal, 0)
    pl.semaphore_wait(barrier, len(peers))

    def near(turn, i):
        for piece in range(1 + turn):
            halo(turn, 1 - core, piece, i).start()

    def far(turn):
        def left(t, carry):
            for piece in range(1 + turn):
                halo(turn, 1 - core, piece, 1 - turn + t).wait_send()
            return carry

        lax.fori_loop(0, half - 1, left, 0)

        def go(i, carry):
            for piece in range(1 + turn):
                halo(turn, core, piece, i).start()
            return carry

        lax.fori_loop(0, half, go, 0)

    def greet(t, carry):
        near(0, half - 1 - t)
        share(0, half - 1 - t).start()
        return carry

    lax.fori_loop(0, half, greet, 0)

    def intake(d):
        wait_side(0, core, depth - d + core * (2 * d - 1 - depth))
        intake_planes[d - 1, 1] = coarse(intake_planes[d - 1, 0])
        share_side(d).start()
        level0[0, depth - d + core * (depth + 2 * d - 1)] = intake_planes[d - 1, core]

    def step(past, to, level, d):
        for z in (depth - d + level, 2 * depth - 1 + d - level):
            v = past[z]
            r = planar_sum(v) + (past[z - 1] + past[z + 1])
            a, h, b = level_coef[level, 0], level_coef[level, 1], level_coef[level, 2]
            to[z] = v * (a - h * (v * v)) + b * r

    def diagonal(turn, d, top):
        step(level0.at[turn], odd, 1, d)

        def two(m, carry):
            step(odd, even, 2 * m, d)
            step(even, odd, 2 * m + 1, d)
            return carry

        lax.fori_loop(1, (top + 1) // 2, two, 0)
        if top % 2 == 0:
            step(odd, even, top, d)

    def wait_halo(turn, d):
        if turn == 0:
            share_side(d).wait_recv()
        else:
            wait_side(turn, 0, depth - d)
            wait_side(turn, 1, d - 1)

    def finish(turn, i):
        wait_halo(turn, half + 1 + i)
        diagonal(turn, half + 1 + i, FSTEPS)
        share_solved(turn, i).start()
        solved[turn, core, i] = even[depth + mine(i)]

    def relay(turn, i):
        @pl.when(chip > 0)
        def _():
            chain(turn, i).wait_recv()

        g = coarse(state[1 + turn, 0, i])
        share_solved(turn, i).wait_recv()
        state[1 + turn, 1, i] = g + (solved[turn, 0, i] - kept[0, i])
        if turn == 0:
            kept[0, i] = g
            share(1, i).start()
        g = coarse(state[1 + turn, 1, i])
        state[1 + turn, 2, i] = g + (solved[turn, 1, i] - kept[1, i])

        @pl.when(chip < chips - 1)
        def _():
            chain(turn, i).start()

        if turn == 0:
            kept[1, i] = g
            near(1, i)
            level0[1, depth + mine(i)] = state[1, core, i]
        else:
            share_final(i).start()
            for j in range(rows):
                out_ref[0, mine(i), pl.ds(j, 8, stride=rows), :] = state[2, 1 + core, i, j]

    for turn in range(2):

        def own(i, carry):
            share(turn, i).wait_recv()
            return carry

        lax.fori_loop(0, half, own, 0)
        for d in range(2 - half, 1):
            diagonal(turn, d, half - 1 + d)
        far(turn)
        if turn == 0:
            intake(1)
        for d in range(1, half + 1):
            if turn == 0:
                intake(d + 1)
            wait_halo(turn, d)
            diagonal(turn, d, half - 1 + d)
        if turn == 0:
            intake(half + 2)
        finish(turn, 0)

        def late(i, carry):
            if turn == 0:

                @pl.when(i < half - 1)
                def _():
                    intake(half + 2 + i)

            finish(turn, i)
            relay(turn, i - 1)
            return carry

        lax.fori_loop(1, half, late, 0)
        relay(turn, half - 1)

        def sent(i, carry):
            share_solved(turn, i).wait_send()
            return carry

        lax.fori_loop(0, half, sent, 0)

    def gather(i, carry):
        share_final(i).wait_recv()
        for j in range(rows):
            out_ref[0, theirs(i), pl.ds(j, 8, stride=rows), :] = final[i, j]
        return carry

    lax.fori_loop(0, half, gather, 0)

    def drain(i, carry):
        for turn in range(2):
            share_side(1 + turn * half + i).wait_send()
            for piece in range(1 + turn):
                halo(turn, core, piece, i).wait_send()

                @pl.when(i == (half - 1) * turn)
                def _():
                    halo(turn, 1 - core, piece, i).wait_send()

            @pl.when(chip < chips - 1)
            def _():
                chain(turn, i).wait_send()

            share(turn, i).wait_send()
        share_final(i).wait_send()
        return carry

    lax.fori_loop(0, half, drain, 0)


def local(initial_state, fine_steps, sweep_count):
    slices, slabs = lax.axis_size("tm"), lax.axis_size("space")
    depth, height, width = initial_state.shape
    plane = (height // 8, 8, width)
    half = depth // 2
    return pl.pallas_call(
        functools.partial(kernel, slices, slabs),
        out_shape=jax.ShapeDtypeStruct((1, *initial_state.shape), jnp.float32),
        in_specs=[
            pl.BlockSpec(memory_space=pltpu.HBM),
            pl.BlockSpec(memory_space=pltpu.SMEM),
            pl.BlockSpec(memory_space=pltpu.SMEM),
        ],
        out_specs=pl.BlockSpec(memory_space=pltpu.VMEM),
        scratch_shapes=[
            pltpu.VMEM((half, height, width), jnp.float32),
            pltpu.VMEM((2, 3 * depth, *plane), jnp.float32),
            pltpu.VMEM((3 * depth, *plane), jnp.float32),
            pltpu.VMEM((3 * depth, *plane), jnp.float32),
            pltpu.VMEM((depth, 2, *plane), jnp.float32),
            pltpu.VMEM((3, 3, half, *plane), jnp.float32),
            pltpu.VMEM((2, 2, half, *plane), jnp.float32),
            pltpu.VMEM((2, half, *plane), jnp.float32),
            pltpu.VMEM((half, *plane), jnp.float32),
            pltpu.VMEM((FSTEPS + 1, 3, *plane[1:]), jnp.float32),
            pltpu.VMEM((SWEEPS + 1, *plane[1:]), jnp.float32),
            pltpu.SemaphoreType.DMA,
            pltpu.SemaphoreType.DMA((2, 2, 2, half)),
            pltpu.SemaphoreType.DMA((2, 2, depth)),
            pltpu.SemaphoreType.DMA((2, half)),
            pltpu.SemaphoreType.DMA((2, half)),
            pltpu.SemaphoreType.DMA((5, half)),
            pltpu.SemaphoreType.DMA((5, half)),
            pltpu.SemaphoreType.DMA((depth,)),
            pltpu.SemaphoreType.DMA((depth,)),
        ],
        compiler_params=pltpu.CompilerParams(
            collective_id=0, has_side_effects=True, vmem_limit_bytes=48 * 1024 * 1024
        ),
    )(initial_state, fine_steps, sweep_count)


def solution(mesh):
    placed = (P("space", None, None), P("tm"), P())
    return jax.shard_map(
        local, mesh=mesh, in_specs=placed, out_specs=P("tm", "space", None, None), check_vma=False
    )
```

```python
import functools

import jax
import jax.numpy as jnp
from jax import lax
from jax.experimental import pallas as pl
from jax.experimental.pallas import tpu as pltpu
from jax.sharding import PartitionSpec as P

FSTEPS = 8
SLICE_TIME = 0.6
MOBILITY = 0.5
WEIGHT = SLICE_TIME * MOBILITY
DIVISOR = 1.0 + 4.0 * WEIGHT
LOWEST_SWEEPS = 2
SWEEPS = 4
MESH = pl.DeviceIdType.MESH


def planar_sum(w):
    last, lanes = w.shape[0] - 1, w.shape[2]
    above = jnp.concatenate([w[1:], pltpu.roll(w[:1], 7, 1)], axis=0)
    below = jnp.concatenate([pltpu.roll(w[last:], 1, 1), w[:last]], axis=0)
    return (above + below) + (pltpu.roll(w, 1, 2) + pltpu.roll(w, lanes - 1, 2))


def row_sum(w):
    lanes = w[0].shape[1]
    above = w[1:] + [pltpu.roll(w[0], 7, 0)]
    below = [pltpu.roll(w[-1], 1, 0)] + w[:-1]
    return [
        (pltpu.roll(w[j], 1, 1) + pltpu.roll(w[j], lanes - 1, 1)) + (above[j] + below[j])
        for j in range(len(w))
    ]


def kernel(slices, slabs, init_ref, fine_ref, sweep_ref, out_ref,
           fetched, level0, odd, even, intake_planes, state, solved, kept, final, level_coef, sweep_coef, fetch_sem,
           halo_send, halo_recv, chain_send, chain_recv, pair_send, pair_recv,
           side_send, side_recv):
    pos = lax.axis_index("tm")
    slab = lax.axis_index("space")
    chip, core = pos // 2, pos % 2
    chips = slices // 2
    depth = init_ref.shape[0]
    half = depth // 2
    rows = even.shape[1]
    other = pos + 1 - 2 * core

    barrier = pltpu.get_barrier_semaphore()
    above, below = (slab + 1) % slabs, (slab + slabs - 1) % slabs
    peers = (
        {"space": above},
        {"space": below},
        {"space": above, "tm": other},
        {"space": below, "tm": other},
        {"tm": other},
    )
    for peer in peers:
        pl.semaphore_signal(barrier, inc=1, device_id=peer, device_id_type=MESH)

    @pl.when(chip > 0)
    def _():
        pl.semaphore_signal(barrier, inc=1, device_id={"tm": pos - 2}, device_id_type=MESH)

    @pl.when(chip < chips - 1)
    def _():
        pl.semaphore_signal(barrier, inc=1, device_id={"tm": pos + 2}, device_id_type=MESH)


    fetch = pltpu.make_async_copy(init_ref.at[pl.ds(half * core, half)], fetched, fetch_sem)
    fetch.start()

    def mine(i):
        return half - 1 - i + core * (1 + 2 * i)

    def theirs(i):
        return half + i - core * (1 + 2 * i)

    def halo(turn, side, piece, i):
        p = mine(i)
        if turn == 0:
            target, core_there = intake_planes.at[depth - 1 - p + side * (2 * p + 1 - depth), 0], side
        else:
            target, core_there = level0.at[1, p + side * (2 * depth)], piece
        return pltpu.make_async_remote_copy(
            src_ref=state.at[turn, piece, i],
            dst_ref=target,
            send_sem=halo_send.at[turn, side, piece, i],
            recv_sem=halo_recv.at[turn, side, p],
            device_id={
                "space": (slab + 1 + side * (slabs - 2)) % slabs,
                "tm": 2 * chip + core_there,
            },
            device_id_type=MESH,
        )

    def wait_side(turn, side, p):
        pltpu.make_async_remote_copy(
            src_ref=state.at[turn, core, 0],
            dst_ref=state.at[turn, core, 0],
            send_sem=halo_send.at[turn, side, 0, 0],
            recv_sem=halo_recv.at[turn, side, p],
            device_id={"space": (slab + 1 + side * (slabs - 2)) % slabs},
            device_id_type=MESH,
        ).wait_recv()

    def share_side(d):
        return pltpu.make_async_remote_copy(
            src_ref=intake_planes.at[d - 1, 1 - core],
            dst_ref=level0.at[0, depth - d + core * (depth + 2 * d - 1)],
            send_sem=side_send.at[d - 1],
            recv_sem=side_recv.at[d - 1],
            device_id={"tm": other},
            device_id_type=MESH,
        )

    def chain(turn, i):
        return pltpu.make_async_remote_copy(
            src_ref=state.at[1 + turn, 2, i],
            dst_ref=state.at[1 + turn, 0, i],
            send_sem=chain_send.at[turn, i],
            recv_sem=chain_recv.at[turn, i],
            device_id={"tm": (pos + 2) % slices},
            device_id_type=MESH,
        )

    def pair(kind, src, dst, i):
        return pltpu.make_async_remote_copy(
            src_ref=src,
            dst_ref=dst,
            send_sem=pair_send.at[kind, i],
            recv_sem=pair_recv.at[kind, i],
            device_id={"tm": other},
            device_id_type=MESH,
        )

    def share(turn, i):
        return pair(turn, state.at[turn, 1 - core, i], level0.at[turn, depth + mine(i)], i)

    def share_solved(turn, i):
        return pair(2 + turn, even.at[depth + theirs(i)], solved.at[turn, core, i], i)

    def share_final(i):
        return pair(4, state.at[2, 2 - core, i], final.at[i], i)

    tile = level_coef.shape[2:]
    count = jnp.full(tile, fine_ref[0], jnp.int32)
    step = SLICE_TIME / count.astype(jnp.float32)
    for level in range(1, FSTEPS + 1):
        h = jnp.where(count >= level, step, 0.0)
        level_coef[level, 0] = 1.0 - 2.0 * h
        level_coef[level, 1] = h
        level_coef[level, 2] = MOBILITY * h
    sweeps = jnp.full(tile, sweep_ref[0], jnp.int32)
    for power in range(SWEEPS + 1):
        factor = (WEIGHT / DIVISOR) ** power
        inner = jnp.where(sweeps > power, factor / DIVISOR, 0.0)
        sweep_coef[power] = jnp.where(sweeps == power, factor, inner)

    def coarse(v):
        power = [v[j] * ((1.0 + SLICE_TIME) - SLICE_TIME * (v[j] * v[j])) for j in range(rows)]
        total = [sweep_coef[0] * x for x in power]
        for turn in range(SWEEPS):
            power = row_sum(power)
            total = [t + sweep_coef[turn + 1] * x for t, x in zip(total, power)]
        return jnp.stack(total)

    def load(i, carry):
        for j in range(rows):
            state[0, 0, i, j] = fetched[mine(i) - half * core, pl.ds(j, 8, stride=rows), :]

        @pl.when(chip == 0)
        def _():
            state[1, 0, i] = state[0, 0, i]
            state[2, 0, i] = state[0, 0, i]

        return carry

    fetch.wait()
    lax.fori_loop(0, half, load, 0)

    def start(n, carry):
        def plane(i, carry):
            state[0, 0, i] = coarse(state[0, 0, i])
            return carry

        return lax.fori_loop(0, half, plane, carry)

    lax.fori_loop(0, 2 * chip, start, 0)
    def deal(i, carry):
        g = coarse(state[0, 0, i])
        state[0, 1, i] = g
        kept[0, i] = g
        level0[0, depth + mine(i)] = state[0, core, i]
        kept[1, i] = coarse(g)
        return carry

    lax.fori_loop(0, half, deal, 0)
    ends = 1 - (chip + chips - 1) // chips + chip // (chips - 1)
    pl.semaphore_wait(barrier, len(peers) + 2 - ends)

    def far(turn):
        def left(t, carry):
            for piece in range(1 + turn):
                halo(turn, 1 - core, piece, 1 - turn + t).wait_send()
            return carry

        lax.fori_loop(0, half - 1, left, 0)

        def go(i, carry):
            for piece in range(1 + turn):
                halo(turn, core, piece, i).start()
            return carry

        lax.fori_loop(0, half, go, 0)

    def greet(t, carry):
        halo(0, 1 - core, 0, half - 1 - t).start()
        share(0, half - 1 - t).start()
        return carry

    lax.fori_loop(0, half, greet, 0)

    def intake(d):
        wait_side(0, core, depth - d + core * (2 * d - 1 - depth))
        intake_planes[d - 1, 1] = coarse(intake_planes[d - 1, 0])
        share_side(d).start()
        level0[0, depth - d + core * (depth + 2 * d - 1)] = intake_planes[d - 1, core]

    def step(past, to, level, d):
        for z in (depth - d + level, 2 * depth - 1 + d - level):
            v = past[z]
            r = planar_sum(v) + (past[z - 1] + past[z + 1])
            a, h, b = level_coef[level, 0], level_coef[level, 1], level_coef[level, 2]
            to[z] = v * (a - h * (v * v)) + b * r

    def diagonal(turn, d, top):
        step(level0.at[turn], odd, 1, d)

        def two(m, carry):
            step(odd, even, 2 * m, d)
            step(even, odd, 2 * m + 1, d)
            return carry

        lax.fori_loop(1, (top + 1) // 2, two, 0)
        if top % 2 == 0:
            step(odd, even, top, d)

    def wait_halo(turn, d):
        if turn == 0:
            share_side(d).wait_recv()
        else:
            wait_side(turn, 0, depth - d)
            wait_side(turn, 1, d - 1)

    def finish(turn, i):
        wait_halo(turn, half + 1 + i)
        diagonal(turn, half + 1 + i, FSTEPS)
        share_solved(turn, i).start()
        solved[turn, core, i] = even[depth + mine(i)]

    def relay(turn, i):
        @pl.when(chip > 0)
        def _():
            chain(turn, i).wait_recv()

        if turn == 0:
            halo(1, 1 - core, 0, i).start()
        g = coarse(state[1 + turn, 0, i])
        share_solved(turn, i).wait_recv()
        state[1 + turn, 1, i] = g + (solved[turn, 0, i] - kept[0, i])
        if turn == 0:
            halo(1, 1 - core, 1, i).start()
            share(1, i).start()
            kept[0, i] = g
        g = coarse(state[1 + turn, 1, i])
        state[1 + turn, 2, i] = g + (solved[turn, 1, i] - kept[1, i])

        @pl.when(chip < chips - 1)
        def _():
            chain(turn, i).start()

        if turn == 0:
            kept[1, i] = g
            level0[1, depth + mine(i)] = state[1, core, i]
        else:
            share_final(i).start()
            for j in range(rows):
                out_ref[0, mine(i), pl.ds(j, 8, stride=rows), :] = state[2, 1 + core, i, j]

    for turn in range(2):

        def own(i, carry):
            share(turn, i).wait_recv()
            return carry

        lax.fori_loop(0, half, own, 0)
        if turn == 1:
            far(1)
        for d in range(2 - half, 1):
            diagonal(turn, d, half - 1 + d)
        if turn == 0:
            far(0)
        if turn == 0:
            intake(1)
        for d in range(1, half + 1):
            if turn == 0:
                intake(d + 1)
            wait_halo(turn, d)
            diagonal(turn, d, half - 1 + d)
        if turn == 0:
            intake(half + 2)
        finish(turn, 0)

        def late(i, carry):
            if turn == 0:

                @pl.when(i < half - 1)
                def _():
                    intake(half + 2 + i)

            finish(turn, i)
            relay(turn, i - 1)
            return carry

        lax.fori_loop(1, half, late, 0)
        relay(turn, half - 1)

        def sent(i, carry):
            share_solved(turn, i).wait_send()
            return carry

        lax.fori_loop(0, half, sent, 0)

    def gather(i, carry):
        share_final(i).wait_recv()
        for j in range(rows):
            out_ref[0, theirs(i), pl.ds(j, 8, stride=rows), :] = final[i, j]
        return carry

    lax.fori_loop(0, half, gather, 0)

    def drain(i, carry):
        for turn in range(2):
            share_side(1 + turn * half + i).wait_send()
            for piece in range(1 + turn):
                halo(turn, core, piece, i).wait_send()

                @pl.when(i == (half - 1) * turn)
                def _():
                    halo(turn, 1 - core, piece, i).wait_send()

            @pl.when(chip < chips - 1)
            def _():
                chain(turn, i).wait_send()

            share(turn, i).wait_send()
        share_final(i).wait_send()
        return carry

    lax.fori_loop(0, half, drain, 0)


def local(initial_state, fine_steps, sweep_count):
    slices, slabs = lax.axis_size("tm"), lax.axis_size("space")
    depth, height, width = initial_state.shape
    plane = (height // 8, 8, width)
    half = depth // 2
    return pl.pallas_call(
        functools.partial(kernel, slices, slabs),
        out_shape=jax.ShapeDtypeStruct((1, *initial_state.shape), jnp.float32),
        in_specs=[
            pl.BlockSpec(memory_space=pltpu.HBM),
            pl.BlockSpec(memory_space=pltpu.SMEM),
            pl.BlockSpec(memory_space=pltpu.SMEM),
        ],
        out_specs=pl.BlockSpec(memory_space=pltpu.VMEM),
        scratch_shapes=[
            pltpu.VMEM((half, height, width), jnp.float32),
            pltpu.VMEM((2, 3 * depth, *plane), jnp.float32),
            pltpu.VMEM((3 * depth, *plane), jnp.float32),
            pltpu.VMEM((3 * depth, *plane), jnp.float32),
            pltpu.VMEM((depth, 2, *plane), jnp.float32),
            pltpu.VMEM((3, 3, half, *plane), jnp.float32),
            pltpu.VMEM((2, 2, half, *plane), jnp.float32),
            pltpu.VMEM((2, half, *plane), jnp.float32),
            pltpu.VMEM((half, *plane), jnp.float32),
            pltpu.VMEM((FSTEPS + 1, 3, *plane[1:]), jnp.float32),
            pltpu.VMEM((SWEEPS + 1, *plane[1:]), jnp.float32),
            pltpu.SemaphoreType.DMA,
            pltpu.SemaphoreType.DMA((2, 2, 2, half)),
            pltpu.SemaphoreType.DMA((2, 2, depth)),
            pltpu.SemaphoreType.DMA((2, half)),
            pltpu.SemaphoreType.DMA((2, half)),
            pltpu.SemaphoreType.DMA((5, half)),
            pltpu.SemaphoreType.DMA((5, half)),
            pltpu.SemaphoreType.DMA((depth,)),
            pltpu.SemaphoreType.DMA((depth,)),
        ],
        compiler_params=pltpu.CompilerParams(
            collective_id=0, has_side_effects=True, vmem_limit_bytes=48 * 1024 * 1024
        ),
    )(initial_state, fine_steps, sweep_count)


def solution(mesh):
    placed = (P("space", None, None), P("tm"), P())
    return jax.shard_map(
        local, mesh=mesh, in_specs=placed, out_specs=P("tm", "space", None, None), check_vma=False
    )
```

```python
import functools

import jax
import jax.numpy as jnp
from jax import lax
from jax.experimental import pallas as pl
from jax.experimental.pallas import tpu as pltpu
from jax.sharding import PartitionSpec as P

FSTEPS = 8
SLICE_TIME = 0.6
MOBILITY = 0.5
WEIGHT = SLICE_TIME * MOBILITY
DIVISOR = 1.0 + 4.0 * WEIGHT
LOWEST_SWEEPS = 2
SWEEPS = 4
MESH = pl.DeviceIdType.MESH


def planar_sum(w):
    last, lanes = w.shape[0] - 1, w.shape[2]
    above = jnp.concatenate([w[1:], pltpu.roll(w[:1], 7, 1)], axis=0)
    below = jnp.concatenate([pltpu.roll(w[last:], 1, 1), w[:last]], axis=0)
    return (above + below) + (pltpu.roll(w, 1, 2) + pltpu.roll(w, lanes - 1, 2))


def row_sum(w):
    lanes = w[0].shape[1]
    above = w[1:] + [pltpu.roll(w[0], 7, 0)]
    below = [pltpu.roll(w[-1], 1, 0)] + w[:-1]
    return [
        (pltpu.roll(w[j], 1, 1) + pltpu.roll(w[j], lanes - 1, 1)) + (above[j] + below[j])
        for j in range(len(w))
    ]


def kernel(slices, slabs, init_ref, fine_ref, sweep_ref, out_ref,
           fetched, level0, odd, even, intake_planes, state, solved, kept, final, level_coef, sweep_coef, fetch_sem,
           halo_send, halo_recv, chain_send, chain_recv, pair_send, pair_recv,
           side_send, side_recv):
    pos = lax.axis_index("tm")
    slab = lax.axis_index("space")
    chip, core = pos // 2, pos % 2
    chips = slices // 2
    depth = init_ref.shape[0]
    half = depth // 2
    rows = even.shape[1]
    other = pos + 1 - 2 * core

    barrier = pltpu.get_barrier_semaphore()
    above, below = (slab + 1) % slabs, (slab + slabs - 1) % slabs
    peers = (
        {"space": above},
        {"space": below},
        {"space": above, "tm": other},
        {"space": below, "tm": other},
        {"tm": other},
    )
    for peer in peers:
        pl.semaphore_signal(barrier, inc=1, device_id=peer, device_id_type=MESH)

    @pl.when(chip > 0)
    def _():
        pl.semaphore_signal(barrier, inc=1, device_id={"tm": pos - 2}, device_id_type=MESH)

    @pl.when(chip < chips - 1)
    def _():
        pl.semaphore_signal(barrier, inc=1, device_id={"tm": pos + 2}, device_id_type=MESH)


    fetch = pltpu.make_async_copy(init_ref.at[pl.ds(half * core, half)], fetched, fetch_sem)
    fetch.start()

    def mine(i):
        return half - 1 - i + core * (1 + 2 * i)

    def theirs(i):
        return half + i - core * (1 + 2 * i)

    def halo(turn, side, piece, i):
        p = mine(i)
        if turn == 0:
            target, core_there = intake_planes.at[depth - 1 - p + side * (2 * p + 1 - depth), 0], side
        else:
            target, core_there = level0.at[1, p + side * (2 * depth)], piece
        return pltpu.make_async_remote_copy(
            src_ref=state.at[turn, piece, i],
            dst_ref=target,
            send_sem=halo_send.at[turn, side, piece, i],
            recv_sem=halo_recv.at[turn, side, p],
            device_id={
                "space": (slab + 1 + side * (slabs - 2)) % slabs,
                "tm": 2 * chip + core_there,
            },
            device_id_type=MESH,
        )

    def wait_side(turn, side, p):
        pltpu.make_async_remote_copy(
            src_ref=state.at[turn, core, 0],
            dst_ref=state.at[turn, core, 0],
            send_sem=halo_send.at[turn, side, 0, 0],
            recv_sem=halo_recv.at[turn, side, p],
            device_id={"space": (slab + 1 + side * (slabs - 2)) % slabs},
            device_id_type=MESH,
        ).wait_recv()

    def share_side(d):
        return pltpu.make_async_remote_copy(
            src_ref=intake_planes.at[d - 1, 1 - core],
            dst_ref=level0.at[0, depth - d + core * (depth + 2 * d - 1)],
            send_sem=side_send.at[d - 1],
            recv_sem=side_recv.at[d - 1],
            device_id={"tm": other},
            device_id_type=MESH,
        )

    def chain(turn, i):
        return pltpu.make_async_remote_copy(
            src_ref=state.at[1 + turn, 2, i],
            dst_ref=state.at[1 + turn, 0, i],
            send_sem=chain_send.at[turn, i],
            recv_sem=chain_recv.at[turn, i],
            device_id={"tm": (pos + 2) % slices},
            device_id_type=MESH,
        )

    def pair(kind, src, dst, i):
        return pltpu.make_async_remote_copy(
            src_ref=src,
            dst_ref=dst,
            send_sem=pair_send.at[kind, i],
            recv_sem=pair_recv.at[kind, i],
            device_id={"tm": other},
            device_id_type=MESH,
        )

    def share(turn, i):
        return pair(turn, state.at[turn, 1 - core, i], level0.at[turn, depth + mine(i)], i)

    def share_solved(turn, i):
        return pair(2 + turn, even.at[depth + theirs(i)], solved.at[turn, core, i], i)

    def share_final(i):
        return pair(4, state.at[2, 2 - core, i], final.at[i], i)

    tile = level_coef.shape[2:]
    count = jnp.full(tile, fine_ref[0], jnp.int32)
    step = SLICE_TIME / count.astype(jnp.float32)
    for level in range(1, FSTEPS + 1):
        h = jnp.where(count >= level, step, 0.0)
        level_coef[level, 0] = 1.0 - 2.0 * h
        level_coef[level, 1] = h
        level_coef[level, 2] = MOBILITY * h
    sweeps = jnp.full(tile, sweep_ref[0], jnp.int32)
    for power in range(SWEEPS + 1):
        factor = (WEIGHT / DIVISOR) ** power
        inner = jnp.where(sweeps > power, factor / DIVISOR, 0.0)
        sweep_coef[power] = jnp.where(sweeps == power, factor, inner)

    def coarse(v):
        power = [v[j] * ((1.0 + SLICE_TIME) - SLICE_TIME * (v[j] * v[j])) for j in range(rows)]
        total = [sweep_coef[0] * x for x in power]
        for turn in range(SWEEPS):
            power = row_sum(power)
            total = [t + sweep_coef[turn + 1] * x for t, x in zip(total, power)]
        return jnp.stack(total)

    def load(i, carry):
        for j in range(rows):
            state[0, 0, i, j] = fetched[mine(i) - half * core, pl.ds(j, 8, stride=rows), :]

        @pl.when(chip == 0)
        def _():
            state[1, 0, i] = state[0, 0, i]
            state[2, 0, i] = state[0, 0, i]

        return carry

    fetch.wait()
    lax.fori_loop(0, half, load, 0)

    def start(n, carry):
        def plane(i, carry):
            state[0, 0, i] = coarse(state[0, 0, i])
            return carry

        return lax.fori_loop(0, half, plane, carry)

    lax.fori_loop(0, 2 * chip, start, 0)
    def deal(i, carry):
        g = coarse(state[0, 0, i])
        state[0, 1, i] = g
        kept[0, i] = g
        level0[0, depth + mine(i)] = state[0, core, i]
        kept[1, i] = coarse(g)
        return carry

    lax.fori_loop(0, half, deal, 0)
    ends = 1 - (chip + chips - 1) // chips + chip // (chips - 1)
    pl.semaphore_wait(barrier, len(peers) + 2 - ends)

    def far(turn):
        def left(t, carry):
            for piece in range(1 + turn):
                halo(turn, 1 - core, piece, 1 - turn + t).wait_send()
            return carry

        lax.fori_loop(0, half - 1, left, 0)

        def go(i, carry):
            for piece in range(1 + turn):
                halo(turn, core, piece, i).start()
            return carry

        lax.fori_loop(0, half, go, 0)

    def greet(t, carry):
        halo(0, 1 - core, 0, half - 1 - t).start()
        share(0, half - 1 - t).start()
        return carry

    lax.fori_loop(0, half, greet, 0)

    def intake(d):
        wait_side(0, core, depth - d + core * (2 * d - 1 - depth))
        intake_planes[d - 1, 1] = coarse(intake_planes[d - 1, 0])
        share_side(d).start()
        level0[0, depth - d + core * (depth + 2 * d - 1)] = intake_planes[d - 1, core]

    def step(past, to, level, d):
        for z in (depth - d + level, 2 * depth - 1 + d - level):
            v = past[z]
            r = planar_sum(v) + (past[z - 1] + past[z + 1])
            a, h, b = level_coef[level, 0], level_coef[level, 1], level_coef[level, 2]
            to[z] = v * (a - h * (v * v)) + b * r

    def diagonal(turn, d, top):
        step(level0.at[turn], odd, 1, d)

        def two(m, carry):
            step(odd, even, 2 * m, d)
            step(even, odd, 2 * m + 1, d)
            return carry

        lax.fori_loop(1, (top + 1) // 2, two, 0)
        if top % 2 == 0:
            step(odd, even, top, d)

    def wait_halo(turn, d):
        if turn == 0:
            share_side(d).wait_recv()
        else:
            wait_side(turn, 0, depth - d)
            wait_side(turn, 1, d - 1)

    def finish(turn, i):
        wait_halo(turn, half + 1 + i)
        diagonal(turn, half + 1 + i, FSTEPS)
        share_solved(turn, i).start()
        solved[turn, core, i] = even[depth + mine(i)]

    def relay(turn, i):
        @pl.when(chip > 0)
        def _():
            chain(turn, i).wait_recv()

        if turn == 0:
            halo(1, 1 - core, 0, i).start()

        @pl.when(chip > 0)
        def _():
            state[1 + turn, 1, i] = coarse(state[1 + turn, 0, i])

        @pl.when(chip == 0)
        def _():
            state[1 + turn, 1, i] = kept[0, i]

        g = state[1 + turn, 1, i]
        share_solved(turn, i).wait_recv()
        state[1 + turn, 1, i] = g + (solved[turn, 0, i] - kept[0, i])
        if turn == 0:
            halo(1, 1 - core, 1, i).start()
            share(1, i).start()
            kept[0, i] = g
        g = coarse(state[1 + turn, 1, i])
        state[1 + turn, 2, i] = g + (solved[turn, 1, i] - kept[1, i])

        @pl.when(chip < chips - 1)
        def _():
            chain(turn, i).start()

        if turn == 0:
            kept[1, i] = g
            level0[1, depth + mine(i)] = state[1, core, i]
        else:
            share_final(i).start()
            for j in range(rows):
                out_ref[0, mine(i), pl.ds(j, 8, stride=rows), :] = state[2, 1 + core, i, j]

    for turn in range(2):

        def own(i, carry):
            share(turn, i).wait_recv()
            return carry

        lax.fori_loop(0, half, own, 0)
        if turn == 1:
            far(1)
        for d in range(2 - half, 1):
            diagonal(turn, d, half - 1 + d)
        if turn == 0:
            far(0)
        if turn == 0:
            intake(1)
        for d in range(1, half + 1):
            if turn == 0:
                intake(d + 1)
            wait_halo(turn, d)
            diagonal(turn, d, half - 1 + d)
        if turn == 0:
            intake(half + 2)
        finish(turn, 0)

        def late(i, carry):
            if turn == 0:

                @pl.when(i < half - 1)
                def _():
                    intake(half + 2 + i)

            finish(turn, i)
            relay(turn, i - 1)
            return carry

        lax.fori_loop(1, half, late, 0)
        relay(turn, half - 1)

        def sent(i, carry):
            share_solved(turn, i).wait_send()
            return carry

        lax.fori_loop(0, half, sent, 0)

    def gather(i, carry):
        share_final(i).wait_recv()
        for j in range(rows):
            out_ref[0, theirs(i), pl.ds(j, 8, stride=rows), :] = final[i, j]
        return carry

    lax.fori_loop(0, half, gather, 0)

    def drain(i, carry):
        for turn in range(2):
            share_side(1 + turn * half + i).wait_send()
            for piece in range(1 + turn):
                halo(turn, core, piece, i).wait_send()

                @pl.when(i == (half - 1) * turn)
                def _():
                    halo(turn, 1 - core, piece, i).wait_send()

            @pl.when(chip < chips - 1)
            def _():
                chain(turn, i).wait_send()

            share(turn, i).wait_send()
        share_final(i).wait_send()
        return carry

    lax.fori_loop(0, half, drain, 0)


def local(initial_state, fine_steps, sweep_count):
    slices, slabs = lax.axis_size("tm"), lax.axis_size("space")
    depth, height, width = initial_state.shape
    plane = (height // 8, 8, width)
    half = depth // 2
    return pl.pallas_call(
        functools.partial(kernel, slices, slabs),
        out_shape=jax.ShapeDtypeStruct((1, *initial_state.shape), jnp.float32),
        in_specs=[
            pl.BlockSpec(memory_space=pltpu.HBM),
            pl.BlockSpec(memory_space=pltpu.SMEM),
            pl.BlockSpec(memory_space=pltpu.SMEM),
        ],
        out_specs=pl.BlockSpec(memory_space=pltpu.VMEM),
        scratch_shapes=[
            pltpu.VMEM((half, height, width), jnp.float32),
            pltpu.VMEM((2, 3 * depth, *plane), jnp.float32),
            pltpu.VMEM((3 * depth, *plane), jnp.float32),
            pltpu.VMEM((3 * depth, *plane), jnp.float32),
            pltpu.VMEM((depth, 2, *plane), jnp.float32),
            pltpu.VMEM((3, 3, half, *plane), jnp.float32),
            pltpu.VMEM((2, 2, half, *plane), jnp.float32),
            pltpu.VMEM((2, half, *plane), jnp.float32),
            pltpu.VMEM((half, *plane), jnp.float32),
            pltpu.VMEM((FSTEPS + 1, 3, *plane[1:]), jnp.float32),
            pltpu.VMEM((SWEEPS + 1, *plane[1:]), jnp.float32),
            pltpu.SemaphoreType.DMA,
            pltpu.SemaphoreType.DMA((2, 2, 2, half)),
            pltpu.SemaphoreType.DMA((2, 2, depth)),
            pltpu.SemaphoreType.DMA((2, half)),
            pltpu.SemaphoreType.DMA((2, half)),
            pltpu.SemaphoreType.DMA((5, half)),
            pltpu.SemaphoreType.DMA((5, half)),
            pltpu.SemaphoreType.DMA((depth,)),
            pltpu.SemaphoreType.DMA((depth,)),
        ],
        compiler_params=pltpu.CompilerParams(
            collective_id=0, has_side_effects=True, vmem_limit_bytes=48 * 1024 * 1024
        ),
    )(initial_state, fine_steps, sweep_count)


def solution(mesh):
    placed = (P("space", None, None), P("tm"), P())
    return jax.shard_map(
        local, mesh=mesh, in_specs=placed, out_specs=P("tm", "space", None, None), check_vma=False
    )
```
